512 devices in a mesh: node: 32 (over z_hi, y), blk: 16 (over x, z_lo, core).
Axes of the slice: x: 4, y: 8, z: 8 (z_hi: 4, z_lo: 2; z = z_hi * 2 + z_lo), core: 2. Of those that a mesh axis runs over, the one named last changes fastest.
Arguments:
- features: bfloat16 [131072, 128], P(('node', 'blk')), may hold values from -6 to 6
- w_one: bfloat16 [128, 256], replicated, may hold values from -0.5 to 0.5
- w_two: bfloat16 [256, 128], replicated, may hold values from -0.75 to 0.75
- tile_values: bfloat16 [32, 16, 128, 128, 128], P('node', 'blk'), may hold values from -0.0625 to 0.0625
- tile_row: int32 [32, 16, 128], P('node', 'blk'), may hold values from 0 to 31
- tile_slot: int32 [32, 16, 128], P('node', 'blk'), may hold values from 0 to 31
- tile_count: int32 [32, 16], P('node', 'blk'), may hold values from 16 to 128, as said below
- send_list: int32 [32, 16, 32], P('node', 'blk'), may hold values from 0 to 1
- cotangent: bfloat16 [131072, 128], P(('node', 'blk')), may hold values from -0.015625 to 0.015625
Outputs:
- logits: bfloat16 [131072, 128], P(('node', 'blk'))
- grad_one: float32 [128, 256], replicated
- grad_two: float32 [256, 128], replicated
The draws below stay inside these ranges and needn't reach their ends.
Inputs may be any that keep to these rules, and one draw needn't show every extreme that they name: `tile_count`: a multiple of 16; some device holds exactly 128 live slots.
All inputs are finite; a program needn't handle non-finite values.
Results may differ from the reference program's by a relative error of at most 0.0065.
Values may be sent and summed in bfloat16 or wider, within the bound.
A program may use at most 64 MiB of HBM per device.

```python
import jax
import jax.numpy as jnp
from jax import lax

F = 128
H = 256
CLS = 128
TILE = 128
GROUP = 16
ROWT = 2
TILES_DEV = 128
NODES = 131072
N_NODE = 32
N_BLK = 16


def draw_tile_count(key, part):
    first_key, second_key = jax.random.split(key)
    groups_full = TILES_DEV // GROUP
    shifts = jax.random.randint(first_key, (N_NODE, N_BLK), 0, 4)
    counted = GROUP * jnp.maximum(1, jnp.right_shift(jnp.int32(groups_full), shifts))
    chosen = jax.random.randint(second_key, (), 0, N_NODE * N_BLK)
    flat = counted.reshape(-1).at[chosen].set(TILES_DEV)
    return flat.reshape(N_NODE, N_BLK).astype(jnp.int32)


def place_ends(drawn, stream_key, low, largest):
    dims = drawn.shape
    index_at = [jax.random.randint(jax.random.fold_in(stream_key, axis), (), 0, dims[axis]) for axis in range(len(dims))]
    drawn = drawn.at[tuple(index_at)].set(low)
    longest = dims.index(max(dims))
    index_at[longest] = (index_at[longest] + 1) % dims[longest]
    return drawn.at[tuple(index_at)].set(largest)


def block_scale(key, shape, cuts, low, high):
    def one(axis_at, shards_of):
        draws = jax.random.uniform(jax.random.fold_in(jax.random.fold_in(key, 6), axis_at), (shards_of,), jnp.float32, low / len(cuts), high / len(cuts))
        return jnp.repeat(jnp.exp(draws), shape[axis_at] // shards_of).reshape((-1,) + (1,) * (len(shape) - axis_at - 1))

    factor_of = one(*cuts[0])
    for cut in cuts[1:]:
        factor_of = factor_of * one(*cut)
    return factor_of


def centred(stream_key, shape, spread, limit, cuts=(), kind=jnp.bfloat16):
    loudness = block_scale(stream_key, shape, cuts, -0.22, 0.18) if cuts else 1.0
    entries = jax.random.normal(stream_key, shape, jnp.float32) * spread * loudness
    return jnp.minimum(jnp.maximum(entries, -limit), limit).astype(kind)


def setup_inputs(seed: int = 0) -> dict:
    seeds = jax.random.split(jax.random.key(seed), 10)
    features = centred(seeds[0], (NODES, F), 1.0, 6.0, ((0, 512),))
    w_one = centred(seeds[1], (F, H), F ** -0.5, 0.5)
    w_two = centred(seeds[2], (H, CLS), (H // 4) ** -0.5, 0.75)
    tile_values = centred(seeds[3], (N_NODE, N_BLK, TILES_DEV, TILE, TILE), (TILES_DEV * TILE // ROWT) ** -0.5, 0.0625, ((0, 32), (1, 16)))
    tile_row = place_ends(jax.random.randint(seeds[4], (N_NODE, N_BLK, TILES_DEV), 0, ROWT * N_BLK), jax.random.fold_in(seeds[4], 1), 0, (ROWT * N_BLK) - 1).astype(jnp.int32)
    tile_slot = place_ends(jax.random.randint(seeds[5], (N_NODE, N_BLK, TILES_DEV), 0, N_NODE), jax.random.fold_in(seeds[5], 1), 0, N_NODE - 1).astype(jnp.int32)
    tile_count = draw_tile_count(jax.random.fold_in(seeds[9], 71), 0)
    send_list = place_ends(jax.random.randint(seeds[7], (N_NODE, N_BLK, N_NODE), 0, ROWT), jax.random.fold_in(seeds[7], 1), 0, ROWT - 1).astype(jnp.int32)
    cotangent = centred(seeds[8], (NODES, CLS), NODES ** -0.5, 0.015625, ((0, 512),))
    return dict(features=features, w_one=w_one, w_two=w_two, tile_values=tile_values, tile_row=tile_row, tile_slot=tile_slot, tile_count=tile_count, send_list=send_list, cotangent=cotangent)


def silu_grad(value):
    sigma = jax.nn.sigmoid(value)
    return sigma * (1.0 + value * (1.0 - sigma))

def aggregate(feat_tiles, tile_values, tile_row, tile_slot, tile_count, send_list, transpose):
    width = feat_tiles.shape[-1]
    block_tiles = ROWT * N_BLK

    def visit(running, device):
        node_index = device // N_BLK
        blk_index = device % N_BLK
        values = tile_values[node_index, blk_index].astype(jnp.float32)
        tile_rows = tile_row[node_index, blk_index]
        tile_slots = tile_slot[node_index, blk_index]
        live = (jnp.arange(TILES_DEV) < tile_count[node_index, blk_index]).astype(jnp.float32)
        picked = send_list[tile_slots, blk_index, node_index]
        columns = ((tile_slots * N_BLK + blk_index) * ROWT + picked).astype(jnp.int32)
        targets = (node_index * block_tiles + tile_rows).astype(jnp.int32)
        if transpose:
            inputs = feat_tiles[targets].astype(jnp.float32)
            product = jnp.einsum('kab,kaw->kbw', values, inputs, precision=lax.Precision.HIGHEST)
            running = running.at[columns].add(product * live[:, None, None])
        else:
            inputs = feat_tiles[columns].astype(jnp.float32)
            product = jnp.einsum('kab,kbw->kaw', values, inputs, precision=lax.Precision.HIGHEST)
            running = running.at[targets].add(product * live[:, None, None])
        return (running, None)
    start = jnp.zeros((feat_tiles.shape[0], TILE, width), jnp.float32)
    result, _ = lax.scan(visit, start, jnp.arange(N_NODE * N_BLK, dtype=jnp.int32))
    return result

def reference(features, w_one, w_two, tile_values, tile_row, tile_slot, tile_count, send_list, cotangent):
    count_tiles = NODES // TILE
    graph = (tile_values, tile_row, tile_slot, tile_count, send_list)
    s_one = aggregate(features.reshape(count_tiles, TILE, F), *graph, False).reshape(NODES, F).astype(jnp.bfloat16)
    z_one = jnp.dot(s_one, w_one, preferred_element_type=jnp.float32)
    h_one = jax.nn.silu(z_one).astype(jnp.bfloat16)
    p_two = jnp.dot(h_one, w_two, preferred_element_type=jnp.float32).astype(jnp.bfloat16)
    logits = aggregate(p_two.reshape(count_tiles, TILE, CLS), *graph, False).reshape(NODES, CLS).astype(jnp.bfloat16)
    d_p_two = aggregate(cotangent.reshape(count_tiles, TILE, CLS), *graph, True).reshape(NODES, CLS).astype(jnp.bfloat16)
    grad_two = jnp.dot(h_one.T, d_p_two, preferred_element_type=jnp.float32)
    d_h = jnp.dot(d_p_two, w_two.T, preferred_element_type=jnp.float32)
    d_z = (d_h * silu_grad(z_one)).astype(jnp.bfloat16)
    grad_one = jnp.dot(s_one.T, d_z, preferred_element_type=jnp.float32)
    return (logits, grad_one, grad_two)
```

```python
import functools

import jax
import jax.numpy as jnp
from jax import lax
from jax.experimental import pallas as pl
from jax.experimental.pallas import tpu as pltpu
from jax.sharding import PartitionSpec as P

MESH = pl.DeviceIdType.MESH
F32 = jnp.float32
BF16 = jnp.bfloat16
TILE = 128
NY = 8
NZ = 4
NODES = NY * NZ
BLKS = 16
SLOTS = 128
UNROLL = 8


def order_kernel(row_ref, slot_ref, count_ref, pick_ref, out_ref):
    shape = (SLOTS, SLOTS)
    sub = lax.broadcasted_iota(jnp.int32, shape, 0).astype(F32)
    lane = lax.broadcasted_iota(jnp.int32, shape, 1).astype(F32)
    count = count_ref[0, 0].astype(F32)
    row = jnp.broadcast_to(row_ref[...].astype(F32), shape)
    slot = jnp.broadcast_to(slot_ref[...].astype(F32), shape)
    out_ref[...] = jnp.zeros_like(out_ref)
    for base, (own, other) in enumerate(((row, slot), (slot, row))):
        key = jnp.where(lane < count, own, 64.0)
        key_t, other_t = key.T, other.T
        before = (key < key_t) | ((key == key_t) & (lane < sub))
        rank = jnp.sum(before.astype(F32), axis=1, keepdims=True)
        chosen = (rank == lane).astype(F32)
        perm = jnp.sum(chosen * sub, axis=0, keepdims=True)
        partner = jnp.sum(chosen * other_t, axis=0, keepdims=True)
        sorted_key = jnp.sum(chosen * key_t, axis=0, keepdims=True)
        start = jnp.sum((key_t < sorted_key).astype(F32), axis=0, keepdims=True)
        keep = (start != lane[0:1]).astype(F32)
        upto = jnp.sum((key_t <= lane).astype(F32), axis=0, keepdims=True)
        has = jnp.sum((key_t == lane).astype(F32), axis=0, keepdims=True)
        last = jnp.maximum(upto - 1.0, 0.0)
        rows = (perm, partner, keep, last, jnp.minimum(has, 1.0))
        for i, value in enumerate(rows):
            out_ref[8 * base + i : 8 * base + i + 1, :] = value.astype(jnp.int32)
    out_ref[5:6, 0:NODES] = pick_ref[...]


def main_kernel(
    plan,
    feat,
    w_one,
    w_two,
    cot,
    values,
    logits,
    grad_one,
    grad_two,
    vbuf,
    cbuf,
    s1,
    r1,
    r5,
    s6,
    r6,
    s2,
    own2,
    c2,
    x2,
    r2,
    p_two,
    s3,
    r3,
    s4,
    c4,
    x4,
    r4,
    gl,
    gc,
    gh,
    gr,
    gx,
    gf,
    gout,
    vsem,
    send,
    recv,
):
    node, blk = lax.axis_index("node"), lax.axis_index("blk")
    zh, y = node // NY, node % NY
    core = blk % 2
    chip = blk // 2
    mate = chip * 2 + (1 - core)

    def node_peer(i):
        step = i % NY
        dy = (1 - 2 * (step % 2)) * ((step + 1) // 2)
        turn = i // NY
        dz = (1 - 2 * (turn % 2)) * ((turn + 1) // 2)
        return ((zh + dz + NZ) % NZ) * NY + (y + dy + NY) % NY

    def copy(src, dst, which, to_node, to_blk):
        pltpu.make_async_remote_copy(
            src_ref=src,
            dst_ref=dst,
            send_sem=send.at[which],
            recv_sem=recv.at[which],
            device_id=(to_node, to_blk),
            device_id_type=MESH,
        ).start()

    def arrived(ref, which):
        pltpu.make_async_copy(ref, ref, recv.at[which]).wait()

    def left(ref, which):
        pltpu.make_async_copy(ref, ref, send.at[which]).wait()

    load = pltpu.make_async_copy(values, vbuf, vsem)
    load.start()
    barrier = pltpu.get_barrier_semaphore()

    def greet_node(i, carry):
        pl.semaphore_signal(
            barrier, inc=1, device_id=(node_peer(i), blk), device_id_type=MESH
        )
        return carry

    def greet_blk(i, carry):
        pl.semaphore_signal(
            barrier, inc=1, device_id=(node, (blk + i) % BLKS), device_id_type=MESH
        )
        return carry

    lax.fori_loop(1, NODES, greet_node, 0)
    lax.fori_loop(1, BLKS, greet_blk, 0)

    for t in range(2):
        tile = cot[t * TILE : (t + 1) * TILE, :].astype(F32)
        r5[blk, t] = tile.T.astype(BF16)

    def pick_features(d, carry):
        s1[d] = feat[plan[5, d]]
        return carry

    lax.fori_loop(0, NODES, pick_features, 0)
    r1[node] = feat[plan[5, node]]
    pl.semaphore_wait(barrier, NODES - 1 + BLKS - 1)

    zmate = (chip // 2) * 4 + (1 - chip % 2) * 2 + core

    def x_peer(i, zl):
        return ((chip // 2 + i) % 4) * 4 + zl * 2 + core

    copy(r5.at[blk], r5.at[blk], 0, node, zmate)

    def spread_own(i, carry):
        copy(r5.at[blk], r5.at[blk], 1, node, x_peer(i, chip % 2))
        return carry

    lax.fori_loop(1, 4, spread_own, 0)
    copy(r5.at[blk], r5.at[blk], 2, node, mate)

    def send_one(i, carry):
        d = node_peer(i)
        copy(s1.at[d], r1.at[node], 3, d, blk)
        return carry

    lax.fori_loop(1, NODES, send_one, 0)
    arrived(r5.at[0], 0)

    def spread_near(i, carry):
        copy(r5.at[zmate], r5.at[zmate], 1, node, x_peer(i, chip % 2))
        return carry

    lax.fori_loop(1, 4, spread_near, 0)
    copy(r5.at[zmate], r5.at[zmate], 2, node, mate)
    arrived(r5.at[pl.ds(0, 6)], 1)

    def hand_over(i, carry):
        for zl in range(2):
            q = x_peer(i, zl)
            copy(r5.at[q], r5.at[q], 2, node, mate)
        return carry

    lax.fori_loop(1, 4, hand_over, 0)
    load.wait()
    arrived(r5.at[pl.ds(0, 8)], 2)

    def products(base, fetch, transposed):
        def group(g, total):
            for u in range(UNROLL):
                p = g * UNROLL + u
                tile = vbuf[plan[base, p]]
                other = fetch(plan[base + 1, p])
                if transposed:
                    term = jnp.dot(other, tile, preferred_element_type=F32)
                else:
                    term = jnp.dot(tile, other, preferred_element_type=F32)
                total = total * plan[base + 2, p].astype(F32) + term
                cbuf[p] = total
            return total

        lax.fori_loop(0, SLOTS // UNROLL, group, jnp.zeros((TILE, TILE), F32))

    def summed(base, r):
        return cbuf[plan[base + 3, r]] * plan[base + 4, r].astype(F32)

    products(8, lambda r: r5[r // 2, r % 2], True)

    def put_six(a, carry):
        s6[a] = summed(8, a).astype(BF16)
        return carry

    lax.fori_loop(0, NODES, put_six, 0)
    r6[node] = s6[node]
    arrived(r1.at[pl.ds(0, NODES - 1)], 3)

    def send_six(i, carry):
        d = node_peer(i)
        copy(s6.at[d], r6.at[node], 4, d, blk)
        return carry

    lax.fori_loop(1, NODES, send_six, 0)

    def reduce_blk(sbuf, cin, xbuf, rbuf, which):
        def give(q, carry):
            for t in range(2):
                sbuf[q, t] = summed(0, 4 * q + 2 * (1 - core) + t).astype(BF16)
            return carry

        lax.fori_loop(0, 8, give, 0)
        copy(sbuf, cin, which, node, mate)

        def stay(q, carry):
            for t in range(2):
                own2[q, t] = summed(0, 4 * q + 2 * core + t)
            return carry

        lax.fori_loop(0, 8, stay, 0)
        arrived(cin, which)

        def join(q, carry):
            total = own2[q] + cin[q].astype(F32)
            own2[q] = total
            xbuf[q] = total.astype(BF16)
            return carry

        lax.fori_loop(0, 8, join, 0)

        def fan(i, carry):
            d = (chip + i) % 8
            copy(xbuf.at[d], rbuf.at[chip], which + 1, node, d * 2 + core)
            return carry

        lax.fori_loop(1, 8, fan, 0)
        rbuf[chip] = xbuf[chip]
        arrived(rbuf.at[pl.ds(0, 7)], which + 1)
        total = rbuf[0].astype(F32)
        for q in range(1, 8):
            total = total + rbuf[q].astype(F32)
        return total.reshape(2 * TILE, TILE)

    products(0, lambda a: r1[a], False)
    s_one = reduce_blk(s2, c2, x2, r2, 5).astype(BF16)
    z_one = jnp.dot(s_one, w_one[...], preferred_element_type=F32)
    sigma = 1.0 / (1.0 + jnp.exp(-z_one))
    h_one = (z_one * sigma).astype(BF16)
    p_two[...] = (
        jnp.dot(h_one, w_two[...], preferred_element_type=F32)
        .astype(BF16)
        .reshape(2, TILE, TILE)
    )

    def pick_two(d, carry):
        s3[d] = p_two[plan[5, d]]
        return carry

    lax.fori_loop(0, NODES, pick_two, 0)
    r3[node] = p_two[plan[5, node]]

    def send_three(i, carry):
        d = node_peer(i)
        copy(s3.at[d], r3.at[node], 7, d, blk)
        return carry

    lax.fori_loop(1, NODES, send_three, 0)

    arrived(r6.at[pl.ds(0, NODES - 1)], 4)

    def back(b, carry):
        low, high = carry
        term = r6[b].astype(F32)
        mark = plan[5, b].astype(F32)
        return low + term * (1.0 - mark), high + term * mark

    none = jnp.zeros((TILE, TILE), F32)
    low, high = lax.fori_loop(0, NODES, back, (none, none))
    d_p = jnp.concatenate([low.T, high.T], axis=0).astype(BF16)
    g_two = lax.dot_general(
        h_one, d_p, (((0,), (0,)), ((), ())), preferred_element_type=F32
    )
    d_h = lax.dot_general(
        d_p, w_two[...], (((1,), (1,)), ((), ())), preferred_element_type=F32
    )
    d_z = (d_h * (sigma * (1.0 + z_one * (1.0 - sigma)))).astype(BF16)
    g_one = lax.dot_general(
        s_one, d_z, (((0,), (0,)), ((), ())), preferred_element_type=F32
    )
    half = (NODES // 2, 8, TILE)
    gl[0, 0 : NODES // 2] = g_one[:, 0:TILE].reshape(half)
    gl[0, NODES // 2 : NODES] = g_one[:, TILE : 2 * TILE].reshape(half)
    gl[1, 0 : NODES // 2] = g_two[0:TILE].reshape(half)
    gl[1, NODES // 2 : NODES] = g_two[TILE : 2 * TILE].reshape(half)
    copy(gl.at[1 - core], gc, 8, node, mate)
    arrived(gc, 8)
    gh[...] = gl[core] + gc[...]

    def send_part(i, carry):
        d = node_peer(i)
        copy(gh.at[d], gr.at[node], 9, d, blk)
        return carry

    lax.fori_loop(1, NODES, send_part, 0)
    gr[node] = gh[node]
    arrived(gr.at[pl.ds(0, NODES - 1)], 9)
    gx[chip] = jnp.sum(gr[...], axis=0)

    def send_chip(i, carry):
        d = (chip + i) % 8
        copy(gx.at[chip], gx.at[chip], 10, node, d * 2 + core)
        return carry

    lax.fori_loop(1, 8, send_chip, 0)
    arrived(gx.at[pl.ds(0, 7)], 10)
    gf[...] = jnp.sum(gx[...], axis=0)
    gout[core, node] = gf[...]

    def send_whole(i, carry):
        copy(gf, gout.at[core, node], 11, node_peer(i), blk)
        return carry

    lax.fori_loop(1, NODES, send_whole, 0)

    arrived(r3.at[pl.ds(0, NODES - 1)], 7)
    products(0, lambda a: r3[a], False)
    total = reduce_blk(s4, c4, x4, r4, 12)
    arrived(gout.at[0, pl.ds(0, NODES - 1)], 11)
    copy(gout.at[core], gout.at[core], 14, node, mate)
    logits[...] = total.astype(BF16)
    arrived(gout.at[0], 14)
    flat = (TILE, TILE)
    grad_one[:, 0:TILE] = gout[0, 0 : NODES // 2].reshape(flat)
    grad_one[:, TILE : 2 * TILE] = gout[0, NODES // 2 : NODES].reshape(flat)
    grad_two[0:TILE] = gout[1, 0 : NODES // 2].reshape(flat)
    grad_two[TILE : 2 * TILE] = gout[1, NODES // 2 : NODES].reshape(flat)

    left(r5.at[0], 0)
    left(r5.at[pl.ds(0, 6)], 1)
    left(r5.at[pl.ds(0, 8)], 2)
    left(r1.at[pl.ds(0, NODES - 1)], 3)
    left(r6.at[pl.ds(0, NODES - 1)], 4)
    left(s2, 5)
    left(r2.at[pl.ds(0, 7)], 6)
    left(r3.at[pl.ds(0, NODES - 1)], 7)
    left(gc, 8)
    left(gr.at[pl.ds(0, NODES - 1)], 9)
    left(gx.at[pl.ds(0, 7)], 10)
    left(gout.at[0, pl.ds(0, NODES - 1)], 11)
    left(s4, 12)
    left(r4.at[pl.ds(0, 7)], 13)
    left(gout.at[0], 14)


def body(
    features, w_one, w_two, tile_values, tile_row, tile_slot, tile_count, send_list, cotangent
):
    in_vmem = pl.BlockSpec(memory_space=pltpu.VMEM)
    in_smem = pl.BlockSpec(memory_space=pltpu.SMEM)
    plan = pl.pallas_call(
        order_kernel,
        out_shape=jax.ShapeDtypeStruct((16, SLOTS), jnp.int32),
        in_specs=[in_vmem, in_vmem, in_smem, in_vmem],
        out_specs=in_vmem,
    )(tile_row[0], tile_slot[0], tile_count, send_list[0])

    tiles = lambda n, kind=BF16: pltpu.VMEM((n, TILE, TILE), kind)
    pairs = lambda n, kind=BF16: pltpu.VMEM((n, 2, TILE, TILE), kind)
    parts = lambda *lead: pltpu.VMEM((*lead, 8, TILE), F32)
    scratch = [
        tiles(SLOTS),
        tiles(SLOTS, F32),
        tiles(NODES),
        tiles(NODES),
        pairs(BLKS),
        tiles(NODES),
        tiles(NODES),
        pairs(8),
        pairs(8, F32),
        pairs(8),
        pairs(8),
        pairs(8),
        tiles(2),
        tiles(NODES),
        tiles(NODES),
        pairs(8),
        pairs(8),
        pairs(8),
        pairs(8),
        parts(2, NODES),
        parts(NODES),
        parts(NODES),
        parts(NODES),
        parts(8),
        parts(),
        parts(2, NODES),
        pltpu.SemaphoreType.DMA,
        pltpu.SemaphoreType.DMA((15,)),
        pltpu.SemaphoreType.DMA((15,)),
    ]
    return pl.pallas_call(
        main_kernel,
        out_shape=(
            jax.ShapeDtypeStruct((2 * TILE, TILE), BF16),
            jax.ShapeDtypeStruct((TILE, 2 * TILE), F32),
            jax.ShapeDtypeStruct((2 * TILE, TILE), F32),
        ),
        in_specs=[in_smem, in_vmem, in_vmem, in_vmem, in_vmem, pl.BlockSpec(memory_space=pl.ANY)],
        out_specs=(in_vmem, in_vmem, in_vmem),
        scratch_shapes=scratch,
        compiler_params=pltpu.CompilerParams(
            collective_id=0, has_side_effects=True, vmem_limit_bytes=60 * 1024 * 1024
        ),
    )(
        plan,
        features.reshape(2, TILE, TILE),
        w_one,
        w_two,
        cotangent,
        tile_values[0, 0],
    )


def solution(mesh):
    placed = (
        P(("node", "blk"), None),
        P(),
        P(),
        P("node", "blk", None, None, None),
        P("node", "blk", None),
        P("node", "blk", None),
        P("node", "blk"),
        P("node", "blk", None),
        P(("node", "blk"), None),
    )
    return jax.shard_map(
        body,
        mesh=mesh,
        in_specs=placed,
        out_specs=(P(("node", "blk"), None), P(), P()),
        check_vma=False,
    )
```

```python
import functools

import jax
import jax.numpy as jnp
from jax import lax
from jax.experimental import pallas as pl
from jax.experimental.pallas import tpu as pltpu
from jax.sharding import PartitionSpec as P

MESH = pl.DeviceIdType.MESH
F32 = jnp.float32
BF16 = jnp.bfloat16
TILE = 128
NY = 8
NZ = 4
NODES = NY * NZ
BLKS = 16
SLOTS = 128
UNROLL = 8


def order_kernel(row_ref, slot_ref, count_ref, pick_ref, out_ref):
    shape = (SLOTS, SLOTS)
    sub = lax.broadcasted_iota(jnp.int32, shape, 0).astype(F32)
    lane = lax.broadcasted_iota(jnp.int32, shape, 1).astype(F32)
    count = count_ref[0, 0].astype(F32)
    row = jnp.broadcast_to(row_ref[...].astype(F32), shape)
    slot = jnp.broadcast_to(slot_ref[...].astype(F32), shape)
    out_ref[...] = jnp.zeros_like(out_ref)
    for base, (own, other) in enumerate(((row, slot), (slot, row))):
        key = jnp.where(lane < count, own, 64.0)
        key_t, other_t = key.T, other.T
        before = (key < key_t) | ((key == key_t) & (lane < sub))
        rank = jnp.sum(before.astype(F32), axis=1, keepdims=True)
        chosen = (rank == lane).astype(F32)
        perm = jnp.sum(chosen * sub, axis=0, keepdims=True)
        partner = jnp.sum(chosen * other_t, axis=0, keepdims=True)
        sorted_key = jnp.sum(chosen * key_t, axis=0, keepdims=True)
        start = jnp.sum((key_t < sorted_key).astype(F32), axis=0, keepdims=True)
        keep = (start != lane[0:1]).astype(F32)
        upto = jnp.sum((key_t <= lane).astype(F32), axis=0, keepdims=True)
        has = jnp.sum((key_t == lane).astype(F32), axis=0, keepdims=True)
        last = jnp.maximum(upto - 1.0, 0.0)
        rows = (perm, partner, keep, last, jnp.minimum(has, 1.0))
        for i, value in enumerate(rows):
            out_ref[8 * base + i : 8 * base + i + 1, :] = value.astype(jnp.int32)
    out_ref[5:6, 0:NODES] = pick_ref[...]


def main_kernel(
    plan,
    feat_in,
    w_one_in,
    w_two_in,
    cot_in,
    values,
    logits,
    grad_one,
    grad_two,
    feat,
    w_one,
    w_two,
    cot,
    vbuf,
    cbuf,
    s1,
    r1,
    r5,
    s6,
    r6,
    s2,
    own2,
    c2,
    x2,
    r2,
    p_two,
    s3,
    r3,
    s4,
    c4,
    x4,
    r4,
    gl,
    gc,
    gh,
    gr,
    gx,
    gf,
    gout,
    vsem,
    send,
    recv,
):
    node, blk = lax.axis_index("node"), lax.axis_index("blk")
    zh, y = lax.div(node, NY), lax.rem(node, NY)
    core = lax.rem(blk, 2)
    chip = lax.div(blk, 2)
    x, zl = lax.div(chip, 2), lax.rem(chip, 2)
    mate = chip * 2 + (1 - core)

    def to_node(visit):
        around = [lax.rem(y + dy, NY) for dy in (0, 1, 7, 2, 6, 3, 5, 4)]

        def level(t, carry):
            first = lax.rem(zh + t, NZ) * NY
            for there in around:
                visit(first + there)
            return carry

        for there in around[1:]:
            visit(zh * NY + there)
        lax.fori_loop(1, NZ, level, 0)

    def copy(src, dst, which, node_of, blk_of):
        pltpu.make_async_remote_copy(
            src_ref=src,
            dst_ref=dst,
            send_sem=send.at[which],
            recv_sem=recv.at[which],
            device_id=(node_of, blk_of),
            device_id_type=MESH,
        ).start()

    def arrived(ref, which):
        pltpu.make_async_copy(ref, ref, recv.at[which]).wait()

    def left(ref, which):
        pltpu.make_async_copy(ref, ref, send.at[which]).wait()

    barrier = pltpu.get_barrier_semaphore()

    def greet(node_of, blk_of):
        pl.semaphore_signal(
            barrier, inc=1, device_id=(node_of, blk_of), device_id_type=MESH
        )

    to_node(lambda d: greet(d, blk))

    def greet_blk(i, carry):
        greet(node, lax.rem(blk + i, BLKS))
        return carry

    lax.fori_loop(1, BLKS, greet_blk, 0)

    small = (
        (cot_in, cot),
        (feat_in, feat),
        (w_one_in, w_one),
        (w_two_in, w_two),
        (values, vbuf),
    )
    loads = [
        pltpu.make_async_copy(src, dst, vsem.at[i]) for i, (src, dst) in enumerate(small)
    ]
    for load in loads:
        load.start()
    loads[0].wait()
    for t in range(2):
        tile = cot[t * TILE : (t + 1) * TILE, :].astype(F32)
        r5[blk, t] = tile.T.astype(BF16)
    loads[1].wait()

    def pick_features(d, carry):
        s1[d] = feat[plan[5, d]]
        return carry

    lax.fori_loop(0, NODES, pick_features, 0)
    r1[node] = feat[plan[5, node]]
    loads[2].wait()
    loads[3].wait()
    pl.semaphore_wait(barrier, NODES - 1 + BLKS - 1)

    zmate = x * 4 + (1 - zl) * 2 + core

    def x_peer(i, level):
        return lax.rem(x + i, 4) * 4 + level * 2 + core

    copy(r5.at[blk], r5.at[blk], 0, node, zmate)

    def spread_own(i, carry):
        copy(r5.at[blk], r5.at[blk], 1, node, x_peer(i, zl))
        return carry

    lax.fori_loop(1, 4, spread_own, 0)
    copy(r5.at[blk], r5.at[blk], 2, node, mate)

    to_node(lambda d: copy(s1.at[d], r1.at[node], 3, d, blk))
    arrived(r5.at[0], 0)

    def spread_near(i, carry):
        copy(r5.at[zmate], r5.at[zmate], 1, node, x_peer(i, zl))
        return carry

    lax.fori_loop(1, 4, spread_near, 0)
    copy(r5.at[zmate], r5.at[zmate], 2, node, mate)
    arrived(r5.at[pl.ds(0, 6)], 1)

    def hand_over(i, carry):
        for level in range(2):
            q = x_peer(i, level)
            copy(r5.at[q], r5.at[q], 2, node, mate)
        return carry

    lax.fori_loop(1, 4, hand_over, 0)
    loads[4].wait()
    arrived(r5.at[pl.ds(0, 8)], 2)

    def products(base, fetch, transposed):
        def group(g, total):
            for u in range(UNROLL):
                p = g * UNROLL + u
                tile = vbuf[plan[base, p]]
                other = fetch(plan[base + 1, p])
                if transposed:
                    term = jnp.dot(other, tile, preferred_element_type=F32)
                else:
                    term = jnp.dot(tile, other, preferred_element_type=F32)
                total = total * plan[base + 2, p].astype(F32) + term
                cbuf[p] = total
            return total

        lax.fori_loop(0, SLOTS // UNROLL, group, jnp.zeros((TILE, TILE), F32))

    def summed(base, r):
        return cbuf[plan[base + 3, r]] * plan[base + 4, r].astype(F32)

    products(8, lambda r: r5[lax.div(r, 2), lax.rem(r, 2)], True)

    def put_six(a, carry):
        s6[a] = summed(8, a).astype(BF16)
        return carry

    lax.fori_loop(0, NODES, put_six, 0)
    r6[node] = s6[node]

    to_node(lambda d: copy(s6.at[d], r6.at[node], 4, d, blk))
    arrived(r1.at[pl.ds(0, NODES - 1)], 3)

    def reduce_blk(sbuf, cin, xbuf, rbuf, which, before, between):
        def give(q, carry):
            for t in range(2):
                sbuf[q, t] = summed(0, 4 * q + 2 * (1 - core) + t).astype(BF16)
            return carry

        lax.fori_loop(0, 8, give, 0)
        copy(sbuf, cin, which, node, mate)

        def stay(q, carry):
            for t in range(2):
                own2[q, t] = summed(0, 4 * q + 2 * core + t)
            return carry

        lax.fori_loop(0, 8, stay, 0)
        before()
        arrived(cin, which)

        def join(q, carry):
            total = own2[q] + cin[q].astype(F32)
            own2[q] = total
            xbuf[q] = total.astype(BF16)
            return carry

        lax.fori_loop(0, 8, join, 0)

        def fan(i, carry):
            d = lax.rem(chip + i, 8)
            copy(xbuf.at[d], rbuf.at[chip], which + 1, node, d * 2 + core)
            return carry

        lax.fori_loop(1, 8, fan, 0)
        between()
        arrived(rbuf.at[pl.ds(0, 7)], which + 1)
        total = own2[chip]
        for i in range(1, 8):
            total = total + rbuf[lax.rem(chip + i, 8)].astype(F32)
        return total.reshape(2 * TILE, TILE)

    products(0, lambda a: r1[a], False)
    s_one = reduce_blk(s2, c2, x2, r2, 5, lambda: None, lambda: None).astype(BF16)
    z_one = jnp.dot(s_one, w_one[...], preferred_element_type=F32)
    sigma = 1.0 / (1.0 + jnp.exp(-z_one))
    h_one = (z_one * sigma).astype(BF16)
    p_two[...] = (
        jnp.dot(h_one, w_two[...], preferred_element_type=F32)
        .astype(BF16)
        .reshape(2, TILE, TILE)
    )

    def pick_two(d, carry):
        s3[d] = p_two[plan[5, d]]
        return carry

    lax.fori_loop(0, NODES, pick_two, 0)
    r3[node] = p_two[plan[5, node]]

    to_node(lambda d: copy(s3.at[d], r3.at[node], 7, d, blk))

    arrived(r6.at[pl.ds(0, NODES - 1)], 4)

    def back(b, carry):
        low, high = carry
        term = r6[b].astype(F32)
        mark = plan[5, b].astype(F32)
        return low + term * (1.0 - mark), high + term * mark

    none = jnp.zeros((TILE, TILE), F32)
    low, high = lax.fori_loop(0, NODES, back, (none, none))
    d_p = jnp.concatenate([low.T, high.T], axis=0).astype(BF16)
    g_two = lax.dot_general(
        h_one, d_p, (((0,), (0,)), ((), ())), preferred_element_type=F32
    )
    d_h = lax.dot_general(
        d_p, w_two[...], (((1,), (1,)), ((), ())), preferred_element_type=F32
    )
    d_z = (d_h * (sigma * (1.0 + z_one * (1.0 - sigma)))).astype(BF16)
    g_one = lax.dot_general(
        s_one, d_z, (((0,), (0,)), ((), ())), preferred_element_type=F32
    )
    half = (NODES // 2, 8, TILE)
    gl[0, 0 : NODES // 2] = g_one[:, 0:TILE].reshape(half)
    gl[0, NODES // 2 : NODES] = g_one[:, TILE : 2 * TILE].reshape(half)
    gl[1, 0 : NODES // 2] = g_two[0:TILE].reshape(half)
    gl[1, NODES // 2 : NODES] = g_two[TILE : 2 * TILE].reshape(half)
    copy(gl.at[1 - core], gc, 8, node, mate)
    arrived(gc, 8)
    gh[...] = gl[core] + gc[...]

    to_node(lambda d: copy(gh.at[d], gr.at[node], 9, d, blk))
    gr[node] = gh[node]

    def share_parts():
        arrived(gr.at[pl.ds(0, NODES - 1)], 9)
        gx[chip] = jnp.sum(gr[...], axis=0)

        def send_chip(i, carry):
            d = lax.rem(chip + i, 8)
            copy(gx.at[chip], gx.at[chip], 10, node, d * 2 + core)
            return carry

        lax.fori_loop(1, 8, send_chip, 0)

    def share_whole():
        arrived(gx.at[pl.ds(0, 7)], 10)
        gf[...] = jnp.sum(gx[...], axis=0)
        gout[core, node] = gf[...]

        to_node(lambda d: copy(gf, gout.at[core, node], 11, d, blk))

    arrived(r3.at[pl.ds(0, NODES - 1)], 7)
    products(0, lambda a: r3[a], False)
    total = reduce_blk(s4, c4, x4, r4, 12, share_parts, share_whole)
    logits[...] = total.astype(BF16)
    arrived(gout.at[0, pl.ds(0, NODES - 1)], 11)
    copy(gout.at[core], gout.at[core], 14, node, mate)
    arrived(gout.at[0], 14)
    flat = (TILE, TILE)
    grad_one[:, 0:TILE] = gout[0, 0 : NODES // 2].reshape(flat)
    grad_one[:, TILE : 2 * TILE] = gout[0, NODES // 2 : NODES].reshape(flat)
    grad_two[0:TILE] = gout[1, 0 : NODES // 2].reshape(flat)
    grad_two[TILE : 2 * TILE] = gout[1, NODES // 2 : NODES].reshape(flat)

    left(r5.at[0], 0)
    left(r5.at[pl.ds(0, 6)], 1)
    left(r5.at[pl.ds(0, 8)], 2)
    left(r1.at[pl.ds(0, NODES - 1)], 3)
    left(r6.at[pl.ds(0, NODES - 1)], 4)
    left(s2, 5)
    left(r2.at[pl.ds(0, 7)], 6)
    left(r3.at[pl.ds(0, NODES - 1)], 7)
    left(gc, 8)
    left(gr.at[pl.ds(0, NODES - 1)], 9)
    left(gx.at[pl.ds(0, 7)], 10)
    left(gout.at[0, pl.ds(0, NODES - 1)], 11)
    left(s4, 12)
    left(r4.at[pl.ds(0, 7)], 13)
    left(gout.at[0], 14)


def hand_out(logits_in, one_in, two_in, logits, one, two):
    logits[...] = logits_in[...]
    one[...] = one_in[...]
    two[...] = two_in[...]


def body(
    features, w_one, w_two, tile_values, tile_row, tile_slot, tile_count, send_list, cotangent
):
    in_vmem = pl.BlockSpec(memory_space=pltpu.VMEM)
    in_smem = pl.BlockSpec(memory_space=pltpu.SMEM)
    in_hbm = pl.BlockSpec(memory_space=pltpu.HBM)
    plan = pl.pallas_call(
        order_kernel,
        out_shape=jax.ShapeDtypeStruct((16, SLOTS), jnp.int32),
        in_specs=[in_vmem, in_vmem, in_smem, in_vmem],
        out_specs=in_vmem,
    )(tile_row[0], tile_slot[0], tile_count, send_list[0])

    tiles = lambda n, kind=BF16: pltpu.VMEM((n, TILE, TILE), kind)
    pairs = lambda n, kind=BF16: pltpu.VMEM((n, 2, TILE, TILE), kind)
    parts = lambda *lead: pltpu.VMEM((*lead, 8, TILE), F32)
    scratch = [
        tiles(2),
        pltpu.VMEM((TILE, 2 * TILE), BF16),
        pltpu.VMEM((2 * TILE, TILE), BF16),
        pltpu.VMEM((2 * TILE, TILE), BF16),
        tiles(SLOTS),
        tiles(SLOTS, F32),
        tiles(NODES),
        tiles(NODES),
        pairs(BLKS),
        tiles(NODES),
        tiles(NODES),
        pairs(8),
        pairs(8, F32),
        pairs(8),
        pairs(8),
        pairs(8),
        tiles(2),
        tiles(NODES),
        tiles(NODES),
        pairs(8),
        pairs(8),
        pairs(8),
        pairs(8),
        parts(2, NODES),
        parts(NODES),
        parts(NODES),
        parts(NODES),
        parts(8),
        parts(),
        parts(2, NODES),
        pltpu.SemaphoreType.DMA((5,)),
        pltpu.SemaphoreType.DMA((15,)),
        pltpu.SemaphoreType.DMA((15,)),
    ]
    results = (
        jax.ShapeDtypeStruct((2 * TILE, TILE), BF16),
        jax.ShapeDtypeStruct((TILE, 2 * TILE), F32),
        jax.ShapeDtypeStruct((2 * TILE, TILE), F32),
    )
    found = pl.pallas_call(
        main_kernel,
        out_shape=results,
        in_specs=[in_smem] + [in_hbm] * 5,
        out_specs=(in_vmem,) * 3,
        scratch_shapes=scratch,
        compiler_params=pltpu.CompilerParams(
            collective_id=0, has_side_effects=True, vmem_limit_bytes=60 * 1024 * 1024
        ),
    )(
        plan,
        features.reshape(2, TILE, TILE),
        w_one,
        w_two,
        cotangent,
        tile_values[0, 0],
    )
    return pl.pallas_call(
        hand_out, out_shape=results, in_specs=[in_vmem] * 3, out_specs=(in_vmem,) * 3
    )(*found)


def solution(mesh):
    placed = (
        P(("node", "blk"), None),
        P(),
        P(),
        P("node", "blk", None, None, None),
        P("node", "blk", None),
        P("node", "blk", None),
        P("node", "blk"),
        P("node", "blk", None),
        P(("node", "blk"), None),
    )
    return jax.shard_map(
        body,
        mesh=mesh,
        in_specs=placed,
        out_specs=(P(("node", "blk"), None), P(), P()),
        check_vma=False,
    )
```

```python
import functools

import jax
import jax.numpy as jnp
from jax import lax
from jax.experimental import pallas as pl
from jax.experimental.pallas import tpu as pltpu
from jax.sharding import PartitionSpec as P

MESH = pl.DeviceIdType.MESH
F32 = jnp.float32
BF16 = jnp.bfloat16
TILE = 128
NY = 8
NZ = 4
NODES = NY * NZ
BLKS = 16
SLOTS = 128
UNROLL = 8


def order_kernel(row_ref, slot_ref, count_ref, pick_ref, out_ref):
    shape = (SLOTS, SLOTS)
    sub = lax.broadcasted_iota(jnp.int32, shape, 0).astype(F32)
    lane = lax.broadcasted_iota(jnp.int32, shape, 1).astype(F32)
    count = count_ref[0, 0].astype(F32)
    row = jnp.broadcast_to(row_ref[...].astype(F32), shape)
    slot = jnp.broadcast_to(slot_ref[...].astype(F32), shape)
    out_ref[...] = jnp.zeros_like(out_ref)
    for base, (own, other) in enumerate(((row, slot), (slot, row))):
        key = jnp.where(lane < count, own, 64.0)
        key_t, other_t = key.T, other.T
        before = (key < key_t) | ((key == key_t) & (lane < sub))
        rank = jnp.sum(before.astype(F32), axis=1, keepdims=True)
        chosen = (rank == lane).astype(F32)
        perm = jnp.sum(chosen * sub, axis=0, keepdims=True)
        partner = jnp.sum(chosen * other_t, axis=0, keepdims=True)
        sorted_key = jnp.sum(chosen * key_t, axis=0, keepdims=True)
        start = jnp.sum((key_t < sorted_key).astype(F32), axis=0, keepdims=True)
        keep = (start != lane[0:1]).astype(F32)
        upto = jnp.sum((key_t <= lane).astype(F32), axis=0, keepdims=True)
        has = jnp.sum((key_t == lane).astype(F32), axis=0, keepdims=True)
        last = jnp.maximum(upto - 1.0, 0.0)
        rows = (perm, partner, keep, last, jnp.minimum(has, 1.0))
        for i, value in enumerate(rows):
            out_ref[8 * base + i : 8 * base + i + 1, :] = value.astype(jnp.int32)
    out_ref[5:6, 0:NODES] = pick_ref[...]


def main_kernel(
    plan,
    feat_in,
    w_one_in,
    w_two_in,
    cot_in,
    values,
    logits,
    grad_one,
    grad_two,
    feat,
    w_one,
    w_two,
    cot,
    vbuf,
    cbuf,
    s1,
    r1,
    r5,
    s6,
    r6,
    c6,
    r7,
    marks,
    s2,
    own2,
    c2,
    x2,
    r2,
    p_two,
    s3,
    r3,
    s4,
    c4,
    x4,
    r4,
    gl,
    gc,
    gh,
    gr,
    gx,
    gf,
    gout,
    vsem,
    send,
    recv,
):
    node, blk = lax.axis_index("node"), lax.axis_index("blk")
    zh, y = lax.div(node, NY), lax.rem(node, NY)
    core = lax.rem(blk, 2)
    chip = lax.div(blk, 2)
    x, zl = lax.div(chip, 2), lax.rem(chip, 2)
    mate = chip * 2 + (1 - core)

    def to_node(visit):
        def line(i, carry):
            side = 1 - 2 * lax.rem(i, 2)
            there = lax.rem(y + side * lax.div(i + 1, 2) + NY, NY)
            for dz in (0, 1, 3, 2):
                visit(lax.rem(zh + dz, NZ) * NY + there)
            return carry

        for dz in (1, 3, 2):
            visit(lax.rem(zh + dz, NZ) * NY + y)
        lax.fori_loop(1, NY, line, 0)

    def copy(src, dst, which, node_of, blk_of):
        pltpu.make_async_remote_copy(
            src_ref=src,
            dst_ref=dst,
            send_sem=send.at[which],
            recv_sem=recv.at[which],
            device_id=(node_of, blk_of),
            device_id_type=MESH,
        ).start()

    def arrived(ref, which):
        pltpu.make_async_copy(ref, ref, recv.at[which]).wait()

    def left(ref, which):
        pltpu.make_async_copy(ref, ref, send.at[which]).wait()

    barrier = pltpu.get_barrier_semaphore()

    def greet(node_of, blk_of):
        pl.semaphore_signal(
            barrier, inc=1, device_id=(node_of, blk_of), device_id_type=MESH
        )

    to_node(lambda d: greet(d, blk))

    def greet_blk(i, carry):
        greet(node, lax.rem(blk + i, BLKS))
        return carry

    lax.fori_loop(1, BLKS, greet_blk, 0)

    small = (
        (cot_in, cot),
        (feat_in, feat),
        (w_one_in, w_one),
        (w_two_in, w_two),
        (values, vbuf),
    )
    loads = [
        pltpu.make_async_copy(src, dst, vsem.at[i]) for i, (src, dst) in enumerate(small)
    ]
    for load in loads:
        load.start()
    loads[0].wait()
    for t in range(2):
        tile = cot[t * TILE : (t + 1) * TILE, :].astype(F32)
        r5[blk, t] = tile.T.astype(BF16)
    loads[1].wait()

    def pick_features(d, carry):
        s1[d] = feat[plan[5, d]]
        return carry

    lax.fori_loop(0, NODES, pick_features, 0)
    r1[node] = feat[plan[5, node]]
    place = lax.broadcasted_iota(jnp.int32, (NY, TILE), 0)
    for level in range(NZ):
        mark = jnp.zeros((NY, TILE), F32)
        for there in range(NY):
            mark = jnp.where(place == there, plan[5, level * NY + there].astype(F32), mark)
        marks[zh, level] = mark
    loads[2].wait()
    loads[3].wait()
    pl.semaphore_wait(barrier, NODES - 1 + BLKS - 1)

    zmate = x * 4 + (1 - zl) * 2 + core

    def x_peer(i, level):
        return lax.rem(x + i, 4) * 4 + level * 2 + core

    copy(r5.at[blk], r5.at[blk], 0, node, zmate)

    def spread_own(i, carry):
        copy(r5.at[blk], r5.at[blk], 1, node, x_peer(i, zl))
        return carry

    lax.fori_loop(1, 4, spread_own, 0)
    copy(r5.at[blk], r5.at[blk], 2, node, mate)

    for t in range(1, NZ):
        copy(marks.at[zh], marks.at[zh], 16, lax.rem(zh + t, NZ) * NY + y, blk)
    to_node(lambda d: copy(s1.at[d], r1.at[node], 3, d, blk))
    arrived(r5.at[0], 0)

    def spread_near(i, carry):
        copy(r5.at[zmate], r5.at[zmate], 1, node, x_peer(i, zl))
        return carry

    lax.fori_loop(1, 4, spread_near, 0)
    copy(r5.at[zmate], r5.at[zmate], 2, node, mate)
    arrived(r5.at[pl.ds(0, 6)], 1)

    def hand_over(i, carry):
        for level in range(2):
            q = x_peer(i, level)
            copy(r5.at[q], r5.at[q], 2, node, mate)
        return carry

    lax.fori_loop(1, 4, hand_over, 0)
    loads[4].wait()
    arrived(r5.at[pl.ds(0, 8)], 2)

    def products(base, fetch, transposed):
        def group(g, total):
            for u in range(UNROLL):
                p = g * UNROLL + u
                tile = vbuf[plan[base, p]]
                other = fetch(plan[base + 1, p])
                if transposed:
                    term = jnp.dot(other, tile, preferred_element_type=F32)
                else:
                    term = jnp.dot(tile, other, preferred_element_type=F32)
                total = total * plan[base + 2, p].astype(F32) + term
                cbuf[p] = total
            return total

        lax.fori_loop(0, SLOTS // UNROLL, group, jnp.zeros((TILE, TILE), F32))

    def summed(base, r):
        return cbuf[plan[base + 3, r]] * plan[base + 4, r].astype(F32)

    products(8, lambda r: r5[lax.div(r, 2), lax.rem(r, 2)], True)

    def put_six(a, carry):
        s6[lax.rem(a, NY), lax.div(a, NY)] = summed(8, a).astype(BF16)
        return carry

    lax.fori_loop(0, NODES, put_six, 0)
    r6[y] = s6[y]

    arrived(r1.at[pl.ds(0, NODES - 1)], 3)
    for dy in (1, 7, 2, 6, 3, 5, 4):
        there = lax.rem(y + dy, NY)
        copy(s6.at[there], r6.at[y], 4, zh * NY + there, blk)

    def reduce_blk(sbuf, cin, xbuf, rbuf, which, before, between):
        def give(q, carry):
            for t in range(2):
                sbuf[q, t] = summed(0, 4 * q + 2 * (1 - core) + t).astype(BF16)
            return carry

        lax.fori_loop(0, 8, give, 0)
        copy(sbuf, cin, which, node, mate)

        def stay(q, carry):
            for t in range(2):
                own2[q, t] = summed(0, 4 * q + 2 * core + t)
            return carry

        lax.fori_loop(0, 8, stay, 0)
        before()
        arrived(cin, which)

        def join(q, carry):
            total = own2[q] + cin[q].astype(F32)
            own2[q] = total
            xbuf[q] = total.astype(BF16)
            return carry

        lax.fori_loop(0, 8, join, 0)

        def fan(i, carry):
            d = lax.rem(chip + i, 8)
            copy(xbuf.at[d], rbuf.at[chip], which + 1, node, d * 2 + core)
            return carry

        lax.fori_loop(1, 8, fan, 0)
        between()
        arrived(rbuf.at[pl.ds(0, 7)], which + 1)
        total = own2[chip]
        for i in range(1, 8):
            total = total + rbuf[lax.rem(chip + i, 8)].astype(F32)
        return total.reshape(2 * TILE, TILE)

    products(0, lambda a: r1[a], False)
    s_one = reduce_blk(s2, c2, x2, r2, 5, lambda: None, lambda: None).astype(BF16)
    z_one = jnp.dot(s_one, w_one[...], preferred_element_type=F32)
    sigma = 1.0 / (1.0 + jnp.exp(-z_one))
    h_one = (z_one * sigma).astype(BF16)
    p_two[...] = (
        jnp.dot(h_one, w_two[...], preferred_element_type=F32)
        .astype(BF16)
        .reshape(2, TILE, TILE)
    )

    def pick_two(d, carry):
        s3[d] = p_two[plan[5, d]]
        return carry

    lax.fori_loop(0, NODES, pick_two, 0)
    r3[node] = p_two[plan[5, node]]

    to_node(lambda d: copy(s3.at[d], r3.at[node], 7, d, blk))

    arrived(r6.at[pl.ds(0, NY - 1)], 4)
    arrived(marks.at[pl.ds(0, NZ - 1)], 16)

    def fold(level):
        low = jnp.zeros((TILE, TILE), F32)
        high = low
        chosen = marks[level, zh]
        for there in range(NY):
            term = r6[there, level].astype(F32)
            mark = chosen[there : there + 1, :]
            low = low + term * (1.0 - mark)
            high = high + term * mark
        return low, high

    def pass_on(t, carry):
        level = lax.rem(zh + t, NZ)
        low, high = fold(level)
        c6[level, 0] = low.astype(BF16)
        c6[level, 1] = high.astype(BF16)
        return carry

    def send_level(t, carry):
        level = lax.rem(zh + t, NZ)
        copy(c6.at[level], r7.at[zh], 15, level * NY + y, blk)
        return carry

    lax.fori_loop(1, NZ, pass_on, 0)
    lax.fori_loop(1, NZ, send_level, 0)
    low, high = fold(zh)
    arrived(r7.at[pl.ds(0, NZ - 1)], 15)
    for t in range(1, NZ):
        level = lax.rem(zh + t, NZ)
        low = low + r7[level, 0].astype(F32)
        high = high + r7[level, 1].astype(F32)
    d_p = jnp.concatenate([low.T, high.T], axis=0).astype(BF16)
    g_two = lax.dot_general(
        h_one, d_p, (((0,), (0,)), ((), ())), preferred_element_type=F32
    )
    d_h = lax.dot_general(
        d_p, w_two[...], (((1,), (1,)), ((), ())), preferred_element_type=F32
    )
    d_z = (d_h * (sigma * (1.0 + z_one * (1.0 - sigma)))).astype(BF16)
    g_one = lax.dot_general(
        s_one, d_z, (((0,), (0,)), ((), ())), preferred_element_type=F32
    )
    half = (NODES // 2, 8, TILE)
    gl[0, 0 : NODES // 2] = g_one[:, 0:TILE].reshape(half)
    gl[0, NODES // 2 : NODES] = g_one[:, TILE : 2 * TILE].reshape(half)
    gl[1, 0 : NODES // 2] = g_two[0:TILE].reshape(half)
    gl[1, NODES // 2 : NODES] = g_two[TILE : 2 * TILE].reshape(half)
    copy(gl.at[1 - core], gc, 8, node, mate)
    arrived(gc, 8)
    gh[...] = gl[core] + gc[...]

    to_node(lambda d: copy(gh.at[d], gr.at[node], 9, d, blk))
    gr[node] = gh[node]

    def share_parts():
        arrived(gr.at[pl.ds(0, NODES - 1)], 9)
        gx[chip] = jnp.sum(gr[...], axis=0)

        def send_chip(i, carry):
            d = lax.rem(chip + i, 8)
            copy(gx.at[chip], gx.at[chip], 10, node, d * 2 + core)
            return carry

        lax.fori_loop(1, 8, send_chip, 0)

    def share_whole():
        arrived(gx.at[pl.ds(0, 7)], 10)
        gf[...] = jnp.sum(gx[...], axis=0)
        gout[core, node] = gf[...]

        to_node(lambda d: copy(gf, gout.at[core, node], 11, d, blk))

    arrived(r3.at[pl.ds(0, NODES - 1)], 7)
    products(0, lambda a: r3[a], False)
    total = reduce_blk(s4, c4, x4, r4, 12, share_parts, share_whole)
    logits[...] = total.astype(BF16)
    arrived(gout.at[0, pl.ds(0, NODES - 1)], 11)
    copy(gout.at[core], gout.at[core], 14, node, mate)
    arrived(gout.at[0], 14)
    flat = (TILE, TILE)
    grad_one[:, 0:TILE] = gout[0, 0 : NODES // 2].reshape(flat)
    grad_one[:, TILE : 2 * TILE] = gout[0, NODES // 2 : NODES].reshape(flat)
    grad_two[0:TILE] = gout[1, 0 : NODES // 2].reshape(flat)
    grad_two[TILE : 2 * TILE] = gout[1, NODES // 2 : NODES].reshape(flat)

    left(r5.at[0], 0)
    left(r5.at[pl.ds(0, 6)], 1)
    left(r5.at[pl.ds(0, 8)], 2)
    left(r1.at[pl.ds(0, NODES - 1)], 3)
    left(r6.at[pl.ds(0, NY - 1)], 4)
    left(r7.at[pl.ds(0, NZ - 1)], 15)
    left(marks.at[pl.ds(0, NZ - 1)], 16)
    left(s2, 5)
    left(r2.at[pl.ds(0, 7)], 6)
    left(r3.at[pl.ds(0, NODES - 1)], 7)
    left(gc, 8)
    left(gr.at[pl.ds(0, NODES - 1)], 9)
    left(gx.at[pl.ds(0, 7)], 10)
    left(gout.at[0, pl.ds(0, NODES - 1)], 11)
    left(s4, 12)
    left(r4.at[pl.ds(0, 7)], 13)
    left(gout.at[0], 14)


def hand_out(logits_in, one_in, two_in, logits, one, two):
    logits[...] = logits_in[...]
    one[...] = one_in[...]
    two[...] = two_in[...]


def body(
    features, w_one, w_two, tile_values, tile_row, tile_slot, tile_count, send_list, cotangent
):
    in_vmem = pl.BlockSpec(memory_space=pltpu.VMEM)
    in_smem = pl.BlockSpec(memory_space=pltpu.SMEM)
    in_hbm = pl.BlockSpec(memory_space=pltpu.HBM)
    plan = pl.pallas_call(
        order_kernel,
        out_shape=jax.ShapeDtypeStruct((16, SLOTS), jnp.int32),
        in_specs=[in_vmem, in_vmem, in_smem, in_vmem],
        out_specs=in_vmem,
    )(tile_row[0], tile_slot[0], tile_count, send_list[0])

    tiles = lambda n, kind=BF16: pltpu.VMEM((n, TILE, TILE), kind)
    pairs = lambda n, kind=BF16: pltpu.VMEM((n, 2, TILE, TILE), kind)
    parts = lambda *lead: pltpu.VMEM((*lead, 8, TILE), F32)
    scratch = [
        tiles(2),
        pltpu.VMEM((TILE, 2 * TILE), BF16),
        pltpu.VMEM((2 * TILE, TILE), BF16),
        pltpu.VMEM((2 * TILE, TILE), BF16),
        tiles(SLOTS),
        tiles(SLOTS, F32),
        tiles(NODES),
        tiles(NODES),
        pairs(BLKS),
        pltpu.VMEM((NY, NZ, TILE, TILE), BF16),
        pltpu.VMEM((NY, NZ, TILE, TILE), BF16),
        pairs(NZ),
        pairs(NZ),
        pltpu.VMEM((NZ, NZ, NY, TILE), F32),
        pairs(8),
        pairs(8, F32),
        pairs(8),
        pairs(8),
        pairs(8),
        tiles(2),
        tiles(NODES),
        tiles(NODES),
        pairs(8),
        pairs(8),
        pairs(8),
        pairs(8),
        parts(2, NODES),
        parts(NODES),
        parts(NODES),
        parts(NODES),
        parts(8),
        parts(),
        parts(2, NODES),
        pltpu.SemaphoreType.DMA((5,)),
        pltpu.SemaphoreType.DMA((17,)),
        pltpu.SemaphoreType.DMA((17,)),
    ]
    results = (
        jax.ShapeDtypeStruct((2 * TILE, TILE), BF16),
        jax.ShapeDtypeStruct((TILE, 2 * TILE), F32),
        jax.ShapeDtypeStruct((2 * TILE, TILE), F32),
    )
    found = pl.pallas_call(
        main_kernel,
        out_shape=results,
        in_specs=[in_smem] + [in_hbm] * 5,
        out_specs=(in_vmem,) * 3,
        scratch_shapes=scratch,
        compiler_params=pltpu.CompilerParams(
            collective_id=0, has_side_effects=True, vmem_limit_bytes=60 * 1024 * 1024
        ),
    )(
        plan,
        features.reshape(2, TILE, TILE),
        w_one,
        w_two,
        cotangent,
        tile_values[0, 0],
    )
    return pl.pallas_call(
        hand_out, out_shape=results, in_specs=[in_vmem] * 3, out_specs=(in_vmem,) * 3
    )(*found)


def solution(mesh):
    placed = (
        P(("node", "blk"), None),
        P(),
        P(),
        P("node", "blk", None, None, None),
        P("node", "blk", None),
        P("node", "blk", None),
        P("node", "blk"),
        P("node", "blk", None),
        P(("node", "blk"), None),
    )
    return jax.shard_map(
        body,
        mesh=mesh,
        in_specs=placed,
        out_specs=(P(("node", "blk"), None), P(), P()),
        check_vma=False,
    )
```

```python
import functools

import jax
import jax.numpy as jnp
from jax import lax
from jax.experimental import pallas as pl
from jax.experimental.pallas import tpu as pltpu
from jax.sharding import PartitionSpec as P

MESH = pl.DeviceIdType.MESH
F32 = jnp.float32
BF16 = jnp.bfloat16
TILE = 128
NY = 8
NZ = 4
NODES = NY * NZ
BLKS = 16
SLOTS = 128
UNROLL = 8


def order_kernel(row_ref, slot_ref, count_ref, pick_ref, out_ref):
    shape = (SLOTS, SLOTS)
    sub = lax.broadcasted_iota(jnp.int32, shape, 0).astype(F32)
    lane = lax.broadcasted_iota(jnp.int32, shape, 1).astype(F32)
    count = count_ref[0, 0].astype(F32)
    row = jnp.broadcast_to(row_ref[...].astype(F32), shape)
    slot = jnp.broadcast_to(slot_ref[...].astype(F32), shape)
    out_ref[...] = jnp.zeros_like(out_ref)
    for base, (own, other) in enumerate(((row, slot), (slot, row))):
        key = jnp.where(lane < count, own, 64.0)
        key_t, other_t = key.T, other.T
        before = (key < key_t) | ((key == key_t) & (lane < sub))
        rank = jnp.sum(before.astype(F32), axis=1, keepdims=True)
        chosen = (rank == lane).astype(F32)
        perm = jnp.sum(chosen * sub, axis=0, keepdims=True)
        partner = jnp.sum(chosen * other_t, axis=0, keepdims=True)
        sorted_key = jnp.sum(chosen * key_t, axis=0, keepdims=True)
        start = jnp.sum((key_t < sorted_key).astype(F32), axis=0, keepdims=True)
        keep = (start != lane[0:1]).astype(F32)
        upto = jnp.sum((key_t <= lane).astype(F32), axis=0, keepdims=True)
        has = jnp.sum((key_t == lane).astype(F32), axis=0, keepdims=True)
        last = jnp.maximum(upto - 1.0, 0.0)
        rows = (perm, partner, keep, last, jnp.minimum(has, 1.0))
        for i, value in enumerate(rows):
            out_ref[8 * base + i : 8 * base + i + 1, :] = value.astype(jnp.int32)
    out_ref[5:6, 0:NODES] = pick_ref[...]


def main_kernel(
    plan,
    feat_in,
    w_one_in,
    w_two_in,
    cot_in,
    values,
    logits,
    grad_one,
    grad_two,
    feat,
    w_one,
    w_two,
    cot,
    vbuf,
    cbuf,
    s1,
    r1,
    r5,
    s6,
    r6,
    c6,
    r7,
    marks,
    s2,
    own2,
    c2,
    x2,
    r2,
    p_two,
    s3,
    r3,
    s4,
    c4,
    x4,
    r4,
    gl,
    gc,
    gh,
    gr,
    gx,
    gf,
    gout,
    vsem,
    send,
    recv,
):
    node, blk = lax.axis_index("node"), lax.axis_index("blk")
    zh, y = lax.div(node, NY), lax.rem(node, NY)
    core = lax.rem(blk, 2)
    chip = lax.div(blk, 2)
    x, zl = lax.div(chip, 2), lax.rem(chip, 2)
    mate = chip * 2 + (1 - core)

    def to_node(visit):
        def line(i, carry):
            side = 1 - 2 * lax.rem(i, 2)
            there = lax.rem(y + side * lax.div(i + 1, 2) + NY, NY)
            for dz in (0, 1, 3, 2):
                visit(lax.rem(zh + dz, NZ) * NY + there)
            return carry

        for dz in (1, 3, 2):
            visit(lax.rem(zh + dz, NZ) * NY + y)
        lax.fori_loop(1, NY, line, 0)

    def copy(src, dst, which, node_of, blk_of):
        pltpu.make_async_remote_copy(
            src_ref=src,
            dst_ref=dst,
            send_sem=send.at[which],
            recv_sem=recv.at[which],
            device_id=(node_of, blk_of),
            device_id_type=MESH,
        ).start()

    def arrived(ref, which):
        pltpu.make_async_copy(ref, ref, recv.at[which]).wait()

    def left(ref, which):
        pltpu.make_async_copy(ref, ref, send.at[which]).wait()

    barrier = pltpu.get_barrier_semaphore()

    def greet(node_of, blk_of):
        pl.semaphore_signal(
            barrier, inc=1, device_id=(node_of, blk_of), device_id_type=MESH
        )

    to_node(lambda d: greet(d, blk))

    def greet_blk(i, carry):
        greet(node, lax.rem(blk + i, BLKS))
        return carry

    lax.fori_loop(1, BLKS, greet_blk, 0)

    small = (
        (cot_in, cot),
        (feat_in, feat),
        (w_one_in, w_one),
        (w_two_in, w_two),
        (values, vbuf),
    )
    loads = [
        pltpu.make_async_copy(src, dst, vsem.at[i]) for i, (src, dst) in enumerate(small)
    ]
    for load in loads:
        load.start()
    loads[0].wait()
    for t in range(2):
        tile = cot[t * TILE : (t + 1) * TILE, :].astype(F32)
        r5[blk, t] = tile.T.astype(BF16)
    loads[1].wait()

    def pick_features(d, carry):
        s1[d] = feat[plan[5, d]]
        return carry

    lax.fori_loop(0, NODES, pick_features, 0)
    r1[node] = feat[plan[5, node]]
    place = lax.broadcasted_iota(jnp.int32, (NY, TILE), 0)
    for level in range(NZ):
        mark = jnp.zeros((NY, TILE), F32)
        for there in range(NY):
            mark = jnp.where(place == there, plan[5, level * NY + there].astype(F32), mark)
        marks[zh, level] = mark
    loads[2].wait()
    loads[3].wait()
    pl.semaphore_wait(barrier, NODES - 1 + BLKS - 1)

    zmate = x * 4 + (1 - zl) * 2 + core

    def x_peer(i, level):
        return lax.rem(x + i, 4) * 4 + level * 2 + core

    copy(r5.at[blk], r5.at[blk], 0, node, zmate)

    def spread_own(i, carry):
        copy(r5.at[blk], r5.at[blk], 1, node, x_peer(i, zl))
        return carry

    lax.fori_loop(1, 4, spread_own, 0)
    copy(r5.at[blk], r5.at[blk], 2, node, mate)

    for t in range(1, NZ):
        copy(marks.at[zh], marks.at[zh], 16, lax.rem(zh + t, NZ) * NY + y, blk)

    def send_one(d):
        copy(s1.at[d], r1.at[node], 3, d, blk)

    for dy in (1, 7, 2, 6, 3, 5, 4):
        send_one(zh * NY + lax.rem(y + dy, NY))
    arrived(r5.at[0], 0)

    def spread_near(i, carry):
        copy(r5.at[zmate], r5.at[zmate], 1, node, x_peer(i, zl))
        return carry

    lax.fori_loop(1, 4, spread_near, 0)
    copy(r5.at[zmate], r5.at[zmate], 2, node, mate)
    for dz in (1, 3, 2):
        send_one(lax.rem(zh + dz, NZ) * NY + y)

    def send_line(i, carry):
        side = 1 - 2 * lax.rem(i, 2)
        there = lax.rem(y + side * lax.div(i + 1, 2) + NY, NY)
        for dz in (1, 3, 2):
            send_one(lax.rem(zh + dz, NZ) * NY + there)
        return carry

    lax.fori_loop(1, NY, send_line, 0)
    arrived(r5.at[pl.ds(0, 6)], 1)

    def hand_over(i, carry):
        for level in range(2):
            q = x_peer(i, level)
            copy(r5.at[q], r5.at[q], 2, node, mate)
        return carry

    lax.fori_loop(1, 4, hand_over, 0)
    loads[4].wait()
    arrived(r5.at[pl.ds(0, 8)], 2)

    def products(base, fetch, transposed):
        def group(g, total):
            for u in range(UNROLL):
                p = g * UNROLL + u
                tile = vbuf[plan[base, p]]
                other = fetch(plan[base + 1, p])
                if transposed:
                    term = jnp.dot(other, tile, preferred_element_type=F32)
                else:
                    term = jnp.dot(tile, other, preferred_element_type=F32)
                total = total * plan[base + 2, p].astype(F32) + term
                cbuf[p] = total
            return total

        lax.fori_loop(0, SLOTS // UNROLL, group, jnp.zeros((TILE, TILE), F32))

    def summed(base, r):
        return cbuf[plan[base + 3, r]] * plan[base + 4, r].astype(F32)

    products(8, lambda r: r5[lax.div(r, 2), lax.rem(r, 2)], True)

    def put_six(a, carry):
        s6[lax.rem(a, NY), lax.div(a, NY)] = summed(8, a).astype(BF16)
        return carry

    lax.fori_loop(0, NODES, put_six, 0)
    r6[y] = s6[y]

    for dy in (1, 7, 2, 6, 3, 5, 4):
        there = lax.rem(y + dy, NY)
        copy(s6.at[there], r6.at[y], 4, zh * NY + there, blk)
    arrived(r1.at[pl.ds(0, NODES - 1)], 3)

    def reduce_blk(sbuf, cin, xbuf, rbuf, which, before, between):
        def give(q, carry):
            for t in range(2):
                sbuf[q, t] = summed(0, 4 * q + 2 * (1 - core) + t).astype(BF16)
            return carry

        lax.fori_loop(0, 8, give, 0)
        copy(sbuf, cin, which, node, mate)

        def stay(q, carry):
            for t in range(2):
                own2[q, t] = summed(0, 4 * q + 2 * core + t)
            return carry

        lax.fori_loop(0, 8, stay, 0)
        before()
        arrived(cin, which)

        def join(q, carry):
            total = own2[q] + cin[q].astype(F32)
            own2[q] = total
            xbuf[q] = total.astype(BF16)
            return carry

        lax.fori_loop(0, 8, join, 0)

        def fan(i, carry):
            d = lax.rem(chip + i, 8)
            copy(xbuf.at[d], rbuf.at[chip], which + 1, node, d * 2 + core)
            return carry

        lax.fori_loop(1, 8, fan, 0)
        between()
        arrived(rbuf.at[pl.ds(0, 7)], which + 1)
        total = own2[chip]
        for i in range(1, 8):
            total = total + rbuf[lax.rem(chip + i, 8)].astype(F32)
        return total.reshape(2 * TILE, TILE)

    products(0, lambda a: r1[a], False)
    s_one = reduce_blk(s2, c2, x2, r2, 5, lambda: None, lambda: None).astype(BF16)
    z_one = jnp.dot(s_one, w_one[...], preferred_element_type=F32)
    sigma = 1.0 / (1.0 + jnp.exp(-z_one))
    h_one = (z_one * sigma).astype(BF16)
    p_two[...] = (
        jnp.dot(h_one, w_two[...], preferred_element_type=F32)
        .astype(BF16)
        .reshape(2, TILE, TILE)
    )

    def pick_two(d, carry):
        s3[d] = p_two[plan[5, d]]
        return carry

    lax.fori_loop(0, NODES, pick_two, 0)
    r3[node] = p_two[plan[5, node]]

    to_node(lambda d: copy(s3.at[d], r3.at[node], 7, d, blk))

    arrived(r6.at[pl.ds(0, NY - 1)], 4)
    arrived(marks.at[pl.ds(0, NZ - 1)], 16)

    def fold(level):
        low = jnp.zeros((TILE, TILE), F32)
        high = low
        chosen = marks[level, zh]
        for there in range(NY):
            term = r6[there, level].astype(F32)
            mark = chosen[there : there + 1, :]
            low = low + term * (1.0 - mark)
            high = high + term * mark
        return low, high

    def pass_on(t, carry):
        level = lax.rem(zh + t, NZ)
        low, high = fold(level)
        c6[level, 0] = low.astype(BF16)
        c6[level, 1] = high.astype(BF16)
        return carry

    def send_level(t, carry):
        level = lax.rem(zh + t, NZ)
        copy(c6.at[level], r7.at[zh], 15, level * NY + y, blk)
        return carry

    lax.fori_loop(1, NZ, pass_on, 0)
    lax.fori_loop(1, NZ, send_level, 0)
    low, high = fold(zh)
    arrived(r7.at[pl.ds(0, NZ - 1)], 15)
    for t in range(1, NZ):
        level = lax.rem(zh + t, NZ)
        low = low + r7[level, 0].astype(F32)
        high = high + r7[level, 1].astype(F32)
    d_p = jnp.concatenate([low.T, high.T], axis=0).astype(BF16)
    g_two = lax.dot_general(
        h_one, d_p, (((0,), (0,)), ((), ())), preferred_element_type=F32
    )
    d_h = lax.dot_general(
        d_p, w_two[...], (((1,), (1,)), ((), ())), preferred_element_type=F32
    )
    d_z = (d_h * (sigma * (1.0 + z_one * (1.0 - sigma)))).astype(BF16)
    g_one = lax.dot_general(
        s_one, d_z, (((0,), (0,)), ((), ())), preferred_element_type=F32
    )
    half = (NODES // 2, 8, TILE)
    gl[0, 0 : NODES // 2] = g_one[:, 0:TILE].reshape(half)
    gl[0, NODES // 2 : NODES] = g_one[:, TILE : 2 * TILE].reshape(half)
    gl[1, 0 : NODES // 2] = g_two[0:TILE].reshape(half)
    gl[1, NODES // 2 : NODES] = g_two[TILE : 2 * TILE].reshape(half)
    copy(gl.at[1 - core], gc, 8, node, mate)
    arrived(gc, 8)
    gh[...] = gl[core] + gc[...]

    to_node(lambda d: copy(gh.at[d], gr.at[node], 9, d, blk))
    gr[node] = gh[node]

    def share_parts():
        arrived(gr.at[pl.ds(0, NODES - 1)], 9)
        gx[chip] = jnp.sum(gr[...], axis=0)

        def send_chip(i, carry):
            d = lax.rem(chip + i, 8)
            copy(gx.at[chip], gx.at[chip], 10, node, d * 2 + core)
            return carry

        lax.fori_loop(1, 8, send_chip, 0)

    def share_whole():
        arrived(gx.at[pl.ds(0, 7)], 10)
        gf[...] = jnp.sum(gx[...], axis=0)
        gout[core, node] = gf[...]

        to_node(lambda d: copy(gf, gout.at[core, node], 11, d, blk))

    arrived(r3.at[pl.ds(0, NODES - 1)], 7)
    products(0, lambda a: r3[a], False)
    total = reduce_blk(s4, c4, x4, r4, 12, share_parts, share_whole)
    logits[...] = total.astype(BF16)
    arrived(gout.at[0, pl.ds(0, NODES - 1)], 11)
    copy(gout.at[core], gout.at[core], 14, node, mate)
    arrived(gout.at[0], 14)
    flat = (TILE, TILE)
    grad_one[:, 0:TILE] = gout[0, 0 : NODES // 2].reshape(flat)
    grad_one[:, TILE : 2 * TILE] = gout[0, NODES // 2 : NODES].reshape(flat)
    grad_two[0:TILE] = gout[1, 0 : NODES // 2].reshape(flat)
    grad_two[TILE : 2 * TILE] = gout[1, NODES // 2 : NODES].reshape(flat)

    left(r5.at[0], 0)
    left(r5.at[pl.ds(0, 6)], 1)
    left(r5.at[pl.ds(0, 8)], 2)
    left(r1.at[pl.ds(0, NODES - 1)], 3)
    left(r6.at[pl.ds(0, NY - 1)], 4)
    left(r7.at[pl.ds(0, NZ - 1)], 15)
    left(marks.at[pl.ds(0, NZ - 1)], 16)
    left(s2, 5)
    left(r2.at[pl.ds(0, 7)], 6)
    left(r3.at[pl.ds(0, NODES - 1)], 7)
    left(gc, 8)
    left(gr.at[pl.ds(0, NODES - 1)], 9)
    left(gx.at[pl.ds(0, 7)], 10)
    left(gout.at[0, pl.ds(0, NODES - 1)], 11)
    left(s4, 12)
    left(r4.at[pl.ds(0, 7)], 13)
    left(gout.at[0], 14)


def hand_out(logits_in, one_in, two_in, logits, one, two):
    logits[...] = logits_in[...]
    one[...] = one_in[...]
    two[...] = two_in[...]


def body(
    features, w_one, w_two, tile_values, tile_row, tile_slot, tile_count, send_list, cotangent
):
    in_vmem = pl.BlockSpec(memory_space=pltpu.VMEM)
    in_smem = pl.BlockSpec(memory_space=pltpu.SMEM)
    in_hbm = pl.BlockSpec(memory_space=pltpu.HBM)
    plan = pl.pallas_call(
        order_kernel,
        out_shape=jax.ShapeDtypeStruct((16, SLOTS), jnp.int32),
        in_specs=[in_vmem, in_vmem, in_smem, in_vmem],
        out_specs=in_vmem,
    )(tile_row[0], tile_slot[0], tile_count, send_list[0])

    tiles = lambda n, kind=BF16: pltpu.VMEM((n, TILE, TILE), kind)
    pairs = lambda n, kind=BF16: pltpu.VMEM((n, 2, TILE, TILE), kind)
    parts = lambda *lead: pltpu.VMEM((*lead, 8, TILE), F32)
    scratch = [
        tiles(2),
        pltpu.VMEM((TILE, 2 * TILE), BF16),
        pltpu.VMEM((2 * TILE, TILE), BF16),
        pltpu.VMEM((2 * TILE, TILE), BF16),
        tiles(SLOTS),
        tiles(SLOTS, F32),
        tiles(NODES),
        tiles(NODES),
        pairs(BLKS),
        pltpu.VMEM((NY, NZ, TILE, TILE), BF16),
        pltpu.VMEM((NY, NZ, TILE, TILE), BF16),
        pairs(NZ),
        pairs(NZ),
        pltpu.VMEM((NZ, NZ, NY, TILE), F32),
        pairs(8),
        pairs(8, F32),
        pairs(8),
        pairs(8),
        pairs(8),
        tiles(2),
        tiles(NODES),
        tiles(NODES),
        pairs(8),
        pairs(8),
        pairs(8),
        pairs(8),
        parts(2, NODES),
        parts(NODES),
        parts(NODES),
        parts(NODES),
        parts(8),
        parts(),
        parts(2, NODES),
        pltpu.SemaphoreType.DMA((5,)),
        pltpu.SemaphoreType.DMA((17,)),
        pltpu.SemaphoreType.DMA((17,)),
    ]
    results = (
        jax.ShapeDtypeStruct((2 * TILE, TILE), BF16),
        jax.ShapeDtypeStruct((TILE, 2 * TILE), F32),
        jax.ShapeDtypeStruct((2 * TILE, TILE), F32),
    )
    found = pl.pallas_call(
        main_kernel,
        out_shape=results,
        in_specs=[in_smem] + [in_hbm] * 5,
        out_specs=(in_vmem,) * 3,
        scratch_shapes=scratch,
        compiler_params=pltpu.CompilerParams(
            collective_id=0, has_side_effects=True, vmem_limit_bytes=60 * 1024 * 1024
        ),
    )(
        plan,
        features.reshape(2, TILE, TILE),
        w_one,
        w_two,
        cotangent,
        tile_values[0, 0],
    )
    return pl.pallas_call(
        hand_out, out_shape=results, in_specs=[in_vmem] * 3, out_specs=(in_vmem,) * 3
    )(*found)


def solution(mesh):
    placed = (
        P(("node", "blk"), None),
        P(),
        P(),
        P("node", "blk", None, None, None),
        P("node", "blk", None),
        P("node", "blk", None),
        P("node", "blk"),
        P("node", "blk", None),
        P(("node", "blk"), None),
    )
    return jax.shard_map(
        body,
        mesh=mesh,
        in_specs=placed,
        out_specs=(P(("node", "blk"), None), P(), P()),
        check_vma=False,
    )
```

```python
import functools

import jax
import jax.numpy as jnp
from jax import lax
from jax.experimental import pallas as pl
from jax.experimental.pallas import tpu as pltpu
from jax.sharding import PartitionSpec as P

MESH = pl.DeviceIdType.MESH
F32 = jnp.float32
BF16 = jnp.bfloat16
TILE = 128
NY = 8
NZ = 4
NODES = NY * NZ
BLKS = 16
SLOTS = 128
UNROLL = 16


def order_kernel(row_ref, slot_ref, count_ref, pick_ref, out_ref):
    shape = (SLOTS, SLOTS)
    sub = lax.broadcasted_iota(jnp.int32, shape, 0).astype(F32)
    lane = lax.broadcasted_iota(jnp.int32, shape, 1).astype(F32)
    count = count_ref[0, 0].astype(F32)
    row = jnp.broadcast_to(row_ref[...].astype(F32), shape)
    slot = jnp.broadcast_to(slot_ref[...].astype(F32), shape)
    out_ref[...] = jnp.zeros_like(out_ref)
    for base, (own, other) in enumerate(((row, slot), (slot, row))):
        key = jnp.where(lane < count, own, 64.0)
        key_t, other_t = key.T, other.T
        before = (key < key_t) | ((key == key_t) & (lane < sub))
        rank = jnp.sum(before.astype(F32), axis=1, keepdims=True)
        chosen = (rank == lane).astype(F32)
        perm = jnp.sum(chosen * sub, axis=0, keepdims=True)
        partner = jnp.sum(chosen * other_t, axis=0, keepdims=True)
        sorted_key = jnp.sum(chosen * key_t, axis=0, keepdims=True)
        start = jnp.sum((key_t < sorted_key).astype(F32), axis=0, keepdims=True)
        keep = (start != lane[0:1]).astype(F32)
        upto = jnp.sum((key_t <= lane).astype(F32), axis=0, keepdims=True)
        has = jnp.sum((key_t == lane).astype(F32), axis=0, keepdims=True)
        last = jnp.maximum(upto - 1.0, 0.0)
        rows = (perm, partner, keep, last, jnp.minimum(has, 1.0))
        for i, value in enumerate(rows):
            out_ref[8 * base + i : 8 * base + i + 1, :] = value.astype(jnp.int32)
    out_ref[5:6, 0:NODES] = pick_ref[...]


def main_kernel(
    plan,
    feat_in,
    w_one_in,
    w_two_in,
    cot_in,
    values,
    logits,
    grad_one,
    grad_two,
    feat,
    w_one,
    w_two,
    cot,
    vbuf,
    cbuf,
    s1,
    r1,
    r5,
    s6,
    r6,
    c6,
    r7,
    marks,
    s2,
    own2,
    c2,
    x2,
    r2,
    p_two,
    s3,
    r3,
    s4,
    c4,
    x4,
    r4,
    gl,
    gc,
    gh,
    gr,
    gx,
    gf,
    gout,
    vsem,
    send,
    recv,
):
    node, blk = lax.axis_index("node"), lax.axis_index("blk")
    zh, y = lax.div(node, NY), lax.rem(node, NY)
    core = lax.rem(blk, 2)
    chip = lax.div(blk, 2)
    x, zl = lax.div(chip, 2), lax.rem(chip, 2)
    mate = chip * 2 + (1 - core)

    def to_node(visit):
        def line(i, carry):
            side = 1 - 2 * lax.rem(i, 2)
            there = lax.rem(y + side * lax.div(i + 1, 2) + NY, NY)
            for dz in (0, 1, 3, 2):
                visit(lax.rem(zh + dz, NZ) * NY + there)
            return carry

        for dz in (1, 3, 2):
            visit(lax.rem(zh + dz, NZ) * NY + y)
        lax.fori_loop(1, NY, line, 0)

    def copy(src, dst, which, node_of, blk_of):
        pltpu.make_async_remote_copy(
            src_ref=src,
            dst_ref=dst,
            send_sem=send.at[which],
            recv_sem=recv.at[which],
            device_id=(node_of, blk_of),
            device_id_type=MESH,
        ).start()

    def arrived(ref, which):
        pltpu.make_async_copy(ref, ref, recv.at[which]).wait()

    def left(ref, which):
        pltpu.make_async_copy(ref, ref, send.at[which]).wait()

    barrier = pltpu.get_barrier_semaphore()

    def greet(node_of, blk_of):
        pl.semaphore_signal(
            barrier, inc=1, device_id=(node_of, blk_of), device_id_type=MESH
        )

    to_node(lambda d: greet(d, blk))

    def greet_blk(i, carry):
        greet(node, lax.rem(blk + i, BLKS))
        return carry

    lax.fori_loop(1, BLKS, greet_blk, 0)

    small = (
        (cot_in, cot),
        (feat_in, feat),
        (w_one_in, w_one),
        (w_two_in, w_two),
        (values, vbuf),
    )
    loads = [
        pltpu.make_async_copy(src, dst, vsem.at[i]) for i, (src, dst) in enumerate(small)
    ]
    for load in loads:
        load.start()
    loads[0].wait()
    for t in range(2):
        tile = cot[t * TILE : (t + 1) * TILE, :].astype(F32)
        r5[blk, t] = tile.T.astype(BF16)
    loads[1].wait()

    def pick_features(d, carry):
        s1[d] = feat[plan[5, d]]
        return carry

    lax.fori_loop(0, NODES, pick_features, 0)
    r1[node] = feat[plan[5, node]]
    place = lax.broadcasted_iota(jnp.int32, (NY, TILE), 0)
    for level in range(NZ):
        mark = jnp.zeros((NY, TILE), F32)
        for there in range(NY):
            mark = jnp.where(place == there, plan[5, level * NY + there].astype(F32), mark)
        marks[zh, level] = mark
    loads[2].wait()
    loads[3].wait()
    pl.semaphore_wait(barrier, NODES - 1 + BLKS - 1)

    zmate = x * 4 + (1 - zl) * 2 + core

    def x_peer(i, level):
        return lax.rem(x + i, 4) * 4 + level * 2 + core

    copy(r5.at[blk], r5.at[blk], 0, node, zmate)

    def spread_own(i, carry):
        copy(r5.at[blk], r5.at[blk], 1, node, x_peer(i, zl))
        return carry

    lax.fori_loop(1, 4, spread_own, 0)
    copy(r5.at[blk], r5.at[blk], 2, node, mate)

    for t in range(1, NZ):
        copy(marks.at[zh], marks.at[zh], 16, lax.rem(zh + t, NZ) * NY + y, blk)

    def send_one(d):
        copy(s1.at[d], r1.at[node], 3, d, blk)

    for dy in (1, 7, 2, 6, 3, 5, 4):
        send_one(zh * NY + lax.rem(y + dy, NY))
    arrived(r5.at[0], 0)

    def spread_near(i, carry):
        copy(r5.at[zmate], r5.at[zmate], 1, node, x_peer(i, zl))
        return carry

    lax.fori_loop(1, 4, spread_near, 0)
    copy(r5.at[zmate], r5.at[zmate], 2, node, mate)
    for dz in (1, 3, 2):
        send_one(lax.rem(zh + dz, NZ) * NY + y)

    def send_line(i, carry):
        side = 1 - 2 * lax.rem(i, 2)
        there = lax.rem(y + side * lax.div(i + 1, 2) + NY, NY)
        for dz in (1, 3, 2):
            send_one(lax.rem(zh + dz, NZ) * NY + there)
        return carry

    lax.fori_loop(1, NY, send_line, 0)
    arrived(r5.at[pl.ds(0, 6)], 1)

    def hand_over(i, carry):
        for level in range(2):
            q = x_peer(i, level)
            copy(r5.at[q], r5.at[q], 2, node, mate)
        return carry

    lax.fori_loop(1, 4, hand_over, 0)
    loads[4].wait()
    arrived(r5.at[pl.ds(0, 8)], 2)

    def products(base, fetch, transposed):
        def group(g, total):
            for u in range(UNROLL):
                p = g * UNROLL + u
                tile = vbuf[plan[base, p]]
                other = fetch(plan[base + 1, p])
                if transposed:
                    term = jnp.dot(other, tile, preferred_element_type=F32)
                else:
                    term = jnp.dot(tile, other, preferred_element_type=F32)
                total = total * plan[base + 2, p].astype(F32) + term
                cbuf[p] = total
            return total

        lax.fori_loop(0, SLOTS // UNROLL, group, jnp.zeros((TILE, TILE), F32))

    def summed(base, r):
        return cbuf[plan[base + 3, r]] * plan[base + 4, r].astype(F32)

    products(8, lambda r: r5[lax.div(r, 2), lax.rem(r, 2)], True)

    def put_six(a, carry):
        s6[lax.rem(a, NY), lax.div(a, NY)] = summed(8, a).astype(BF16)
        return carry

    lax.fori_loop(0, NODES, put_six, 0)
    r6[y] = s6[y]

    for dy in (1, 7, 2, 6, 3, 5, 4):
        there = lax.rem(y + dy, NY)
        copy(s6.at[there], r6.at[y], 4, zh * NY + there, blk)
    arrived(r1.at[pl.ds(0, NODES - 1)], 3)

    def reduce_blk(sbuf, cin, xbuf, rbuf, which, before, between):
        def give(q, carry):
            for t in range(2):
                sbuf[q, t] = summed(0, 4 * q + 2 * (1 - core) + t).astype(BF16)
            return carry

        lax.fori_loop(0, 8, give, 0)
        copy(sbuf, cin, which, node, mate)

        def stay(q, carry):
            for t in range(2):
                own2[q, t] = summed(0, 4 * q + 2 * core + t)
            return carry

        lax.fori_loop(0, 8, stay, 0)
        before()
        arrived(cin, which)

        def join(q, carry):
            total = own2[q] + cin[q].astype(F32)
            own2[q] = total
            xbuf[q] = total.astype(BF16)
            return carry

        lax.fori_loop(0, 8, join, 0)

        def fan(i, carry):
            d = lax.rem(chip + i, 8)
            copy(xbuf.at[d], rbuf.at[chip], which + 1, node, d * 2 + core)
            return carry

        lax.fori_loop(1, 8, fan, 0)
        between()
        arrived(rbuf.at[pl.ds(0, 7)], which + 1)
        total = own2[chip]
        for i in range(1, 8):
            total = total + rbuf[lax.rem(chip + i, 8)].astype(F32)
        return total.reshape(2 * TILE, TILE)

    products(0, lambda a: r1[a], False)
    s_one = reduce_blk(s2, c2, x2, r2, 5, lambda: None, lambda: None).astype(BF16)
    z_one = jnp.dot(s_one, w_one[...], preferred_element_type=F32)
    sigma = 1.0 / (1.0 + jnp.exp(-z_one))
    h_one = (z_one * sigma).astype(BF16)
    p_two[...] = (
        jnp.dot(h_one, w_two[...], preferred_element_type=F32)
        .astype(BF16)
        .reshape(2, TILE, TILE)
    )

    def pick_two(d, carry):
        s3[d] = p_two[plan[5, d]]
        return carry

    lax.fori_loop(0, NODES, pick_two, 0)
    r3[node] = p_two[plan[5, node]]

    to_node(lambda d: copy(s3.at[d], r3.at[node], 7, d, blk))

    arrived(r6.at[pl.ds(0, NY - 1)], 4)
    arrived(marks.at[pl.ds(0, NZ - 1)], 16)

    def fold(level):
        low = jnp.zeros((TILE, TILE), F32)
        high = low
        chosen = marks[level, zh]
        for there in range(NY):
            term = r6[there, level].astype(F32)
            mark = chosen[there : there + 1, :]
            low = low + term * (1.0 - mark)
            high = high + term * mark
        return low, high

    def pass_on(t, carry):
        level = lax.rem(zh + t, NZ)
        low, high = fold(level)
        c6[level, 0] = low.astype(BF16)
        c6[level, 1] = high.astype(BF16)
        return carry

    def send_level(t, carry):
        level = lax.rem(zh + t, NZ)
        copy(c6.at[level], r7.at[zh], 15, level * NY + y, blk)
        return carry

    lax.fori_loop(1, NZ, pass_on, 0)
    lax.fori_loop(1, NZ, send_level, 0)
    low, high = fold(zh)
    arrived(r7.at[pl.ds(0, NZ - 1)], 15)
    for t in range(1, NZ):
        level = lax.rem(zh + t, NZ)
        low = low + r7[level, 0].astype(F32)
        high = high + r7[level, 1].astype(F32)
    d_p = jnp.concatenate([low.T, high.T], axis=0).astype(BF16)
    g_two = lax.dot_general(
        h_one, d_p, (((0,), (0,)), ((), ())), preferred_element_type=F32
    )
    d_h = lax.dot_general(
        d_p, w_two[...], (((1,), (1,)), ((), ())), preferred_element_type=F32
    )
    d_z = (d_h * (sigma * (1.0 + z_one * (1.0 - sigma)))).astype(BF16)
    g_one = lax.dot_general(
        s_one, d_z, (((0,), (0,)), ((), ())), preferred_element_type=F32
    )
    half = (NODES // 2, 8, TILE)
    gl[0, 0 : NODES // 2] = g_one[:, 0:TILE].reshape(half)
    gl[0, NODES // 2 : NODES] = g_one[:, TILE : 2 * TILE].reshape(half)
    gl[1, 0 : NODES // 2] = g_two[0:TILE].reshape(half)
    gl[1, NODES // 2 : NODES] = g_two[TILE : 2 * TILE].reshape(half)
    copy(gl.at[1 - core], gc, 8, node, mate)
    arrived(gc, 8)
    gh[...] = gl[core] + gc[...]

    to_node(lambda d: copy(gh.at[d], gr.at[node], 9, d, blk))
    gr[node] = gh[node]

    def share_parts():
        arrived(gr.at[pl.ds(0, NODES - 1)], 9)
        gx[chip] = jnp.sum(gr[...], axis=0)

        def send_chip(i, carry):
            d = lax.rem(chip + i, 8)
            copy(gx.at[chip], gx.at[chip], 10, node, d * 2 + core)
            return carry

        lax.fori_loop(1, 8, send_chip, 0)

    def share_whole():
        arrived(gx.at[pl.ds(0, 7)], 10)
        gf[...] = jnp.sum(gx[...], axis=0)
        gout[core, node] = gf[...]

        to_node(lambda d: copy(gf, gout.at[core, node], 11, d, blk))

    arrived(r3.at[pl.ds(0, NODES - 1)], 7)
    products(0, lambda a: r3[a], False)
    total = reduce_blk(s4, c4, x4, r4, 12, share_parts, share_whole)
    logits[...] = total.astype(BF16)
    arrived(gout.at[0, pl.ds(0, NODES - 1)], 11)
    copy(gout.at[core], gout.at[core], 14, node, mate)
    arrived(gout.at[0], 14)
    flat = (TILE, TILE)
    grad_one[:, 0:TILE] = gout[0, 0 : NODES // 2].reshape(flat)
    grad_one[:, TILE : 2 * TILE] = gout[0, NODES // 2 : NODES].reshape(flat)
    grad_two[0:TILE] = gout[1, 0 : NODES // 2].reshape(flat)
    grad_two[TILE : 2 * TILE] = gout[1, NODES // 2 : NODES].reshape(flat)

    left(r5.at[0], 0)
    left(r5.at[pl.ds(0, 6)], 1)
    left(r5.at[pl.ds(0, 8)], 2)
    left(r1.at[pl.ds(0, NODES - 1)], 3)
    left(r6.at[pl.ds(0, NY - 1)], 4)
    left(r7.at[pl.ds(0, NZ - 1)], 15)
    left(marks.at[pl.ds(0, NZ - 1)], 16)
    left(s2, 5)
    left(r2.at[pl.ds(0, 7)], 6)
    left(r3.at[pl.ds(0, NODES - 1)], 7)
    left(gc, 8)
    left(gr.at[pl.ds(0, NODES - 1)], 9)
    left(gx.at[pl.ds(0, 7)], 10)
    left(gout.at[0, pl.ds(0, NODES - 1)], 11)
    left(s4, 12)
    left(r4.at[pl.ds(0, 7)], 13)
    left(gout.at[0], 14)


def hand_out(logits_in, one_in, two_in, logits, one, two):
    logits[...] = logits_in[...]
    one[...] = one_in[...]
    two[...] = two_in[...]


def body(
    features, w_one, w_two, tile_values, tile_row, tile_slot, tile_count, send_list, cotangent
):
    in_vmem = pl.BlockSpec(memory_space=pltpu.VMEM)
    in_smem = pl.BlockSpec(memory_space=pltpu.SMEM)
    in_hbm = pl.BlockSpec(memory_space=pltpu.HBM)
    plan = pl.pallas_call(
        order_kernel,
        out_shape=jax.ShapeDtypeStruct((16, SLOTS), jnp.int32),
        in_specs=[in_vmem, in_vmem, in_smem, in_vmem],
        out_specs=in_vmem,
    )(tile_row[0], tile_slot[0], tile_count, send_list[0])

    tiles = lambda n, kind=BF16: pltpu.VMEM((n, TILE, TILE), kind)
    pairs = lambda n, kind=BF16: pltpu.VMEM((n, 2, TILE, TILE), kind)
    parts = lambda *lead: pltpu.VMEM((*lead, 8, TILE), F32)
    scratch = [
        tiles(2),
        pltpu.VMEM((TILE, 2 * TILE), BF16),
        pltpu.VMEM((2 * TILE, TILE), BF16),
        pltpu.VMEM((2 * TILE, TILE), BF16),
        tiles(SLOTS),
        tiles(SLOTS, F32),
        tiles(NODES),
        tiles(NODES),
        pairs(BLKS),
        pltpu.VMEM((NY, NZ, TILE, TILE), BF16),
        pltpu.VMEM((NY, NZ, TILE, TILE), BF16),
        pairs(NZ),
        pairs(NZ),
        pltpu.VMEM((NZ, NZ, NY, TILE), F32),
        pairs(8),
        pairs(8, F32),
        pairs(8),
        pairs(8),
        pairs(8),
        tiles(2),
        tiles(NODES),
        tiles(NODES),
        pairs(8),
        pairs(8),
        pairs(8),
        pairs(8),
        parts(2, NODES),
        parts(NODES),
        parts(NODES),
        parts(NODES),
        parts(8),
        parts(),
        parts(2, NODES),
        pltpu.SemaphoreType.DMA((5,)),
        pltpu.SemaphoreType.DMA((17,)),
        pltpu.SemaphoreType.DMA((17,)),
    ]
    results = (
        jax.ShapeDtypeStruct((2 * TILE, TILE), BF16),
        jax.ShapeDtypeStruct((TILE, 2 * TILE), F32),
        jax.ShapeDtypeStruct((2 * TILE, TILE), F32),
    )
    found = pl.pallas_call(
        main_kernel,
        out_shape=results,
        in_specs=[in_smem] + [in_hbm] * 5,
        out_specs=(in_vmem,) * 3,
        scratch_shapes=scratch,
        compiler_params=pltpu.CompilerParams(
            collective_id=0, has_side_effects=True, vmem_limit_bytes=60 * 1024 * 1024
        ),
    )(
        plan,
        features.reshape(2, TILE, TILE),
        w_one,
        w_two,
        cotangent,
        tile_values[0, 0],
    )
    return pl.pallas_call(
        hand_out, out_shape=results, in_specs=[in_vmem] * 3, out_specs=(in_vmem,) * 3
    )(*found)


def solution(mesh):
    placed = (
        P(("node", "blk"), None),
        P(),
        P(),
        P("node", "blk", None, None, None),
        P("node", "blk", None),
        P("node", "blk", None),
        P("node", "blk"),
        P("node", "blk", None),
        P(("node", "blk"), None),
    )
    return jax.shard_map(
        body,
        mesh=mesh,
        in_specs=placed,
        out_specs=(P(("node", "blk"), None), P(), P()),
        check_vma=False,
    )
```
